32 devices in a mesh: dp: 8 (over y, x, core), seq: 4 (over z).
Axes of the slice: x: 2, y: 2, z: 4, core: 2. Of those that a mesh axis runs over, the one named last changes fastest.
Arguments:
- qkv: bfloat16 [16, 1024, 4608], P('dp', 'seq'), may hold values from -20.4 to 20.4
- gate: float32 [16, 3072], P('dp'), may hold values from 0.5 to 2.5
- cotangent: bfloat16 [16, 1024, 3072], P('dp', 'seq'), may hold values from -6 to 6
- out_weight: bfloat16 [1536, 3072], replicated, may hold values from -0.15625 to 0.15625
- clip_lengths: int32 [16], replicated, may hold values from 1 to 768, as said below
- text_lengths: int32 [16], replicated, may hold values from 1 to 256, as said below
- plan: int32 [8], replicated, may hold values from 0 to 7, as said below
Outputs:
- mixed: bfloat16 [16, 1024, 3072], P('dp', 'seq')
- gate_grad: float32 [16, 3072], P('dp')
- weight_grad: float32 [1536, 3072], P(None, ('dp', 'seq'))
- qkv_grad: bfloat16 [16, 1024, 4608], P('dp', 'seq')
The draws below stay inside these ranges and needn't reach their ends.
Inputs may be any that keep to these rules, and one draw needn't show every extreme that they name: clip_lengths[c] counts the live video positions of source clip c = 2 g + s (group g, slot s); some clip has exactly 768. text_lengths[c] counts the live text positions of source clip c; some clip has exactly 256. plan is a permutation of 0 to 7: the second clip of group g becomes the second clip of group plan[g].
All inputs are finite; a program needn't handle non-finite values.
Results may differ from the reference program's by a relative error of at most 0.011.
Values may be sent and summed in bfloat16 or wider, within the bound.
A program may use at most 128 MiB of HBM per device.

```python
import jax
import jax.numpy as jnp
from jax import lax

D = 3072
HEADS = 12
HD = 128
TXT = 256
CLIP = 768
GROUPS = 8
CLIPS = 16
SEQ = 1024


def draw_qkv(key, part):
    head_width = HEADS * HD
    full_width = 3 * head_width
    normal_draw = jnp.clip(jax.random.normal(key, (CLIPS, SEQ, full_width), jnp.float32), -6.0, 6.0)
    return normal_draw.astype(jnp.bfloat16)


def length_table(key):
    folded = jax.random.fold_in(key, 11)
    k_heavy, k_long, k_short, k_peak = jax.random.split(folded, 4)
    heavier = jax.random.randint(k_heavy, (GROUPS, 1), 0, 2)
    longer = jax.random.randint(k_long, (GROUPS, 2), CLIP // 2 + 1, CLIP + 1)
    shorter = jax.random.randint(k_short, (GROUPS, 2), 1, CLIP // 4 + 1)
    lengths_all = jnp.where(heavier == 1, longer, shorter).reshape(CLIPS)
    peak_index = jax.random.randint(k_peak, (), 0, CLIPS)
    return jnp.where(jnp.arange(CLIPS) == peak_index, CLIP, lengths_all).astype(jnp.int32)


def draw_clip_lengths(key, part):
    return length_table(key)


def draw_plan(key, part):
    lengths_all = length_table(key)
    ordinal = jnp.arange(GROUPS, dtype=jnp.int32)
    first_keys = lengths_all[0::2] * GROUPS + ordinal
    second = lengths_all[1::2] * GROUPS + ordinal
    longest = jnp.argsort(-first_keys, stable=True).astype(jnp.int32)
    shortest = jnp.argsort(second, stable=True).astype(jnp.int32)
    return jnp.zeros((GROUPS,), jnp.int32).at[shortest].set(longest)


def draw_text_lengths(key, part):
    folded = jax.random.fold_in(key, 23)
    k_draw, k_peak = jax.random.split(folded, 2)
    lengths_all = jax.random.randint(k_draw, (CLIPS,), 1, TXT + 1)
    peak_index = jax.random.randint(k_peak, (), 0, CLIPS)
    return jnp.where(jnp.arange(CLIPS) == peak_index, TXT, lengths_all).astype(jnp.int32)


def level_of(key, shape, shards, low, top_value):
    def one(position, blocks):
        heights = jax.random.uniform(jax.random.fold_in(jax.random.fold_in(key, 6), position), (blocks,), jnp.float32, low / len(shards), top_value / len(shards))
        return jnp.repeat(jnp.exp(heights), shape[position] // blocks).reshape((-1,) + (1,) * (len(shape) - position - 1))

    gain = one(*shards[0])
    for cut in shards[1:]:
        gain = gain * one(*cut)
    return gain


def bell_draw(stream_key, dims, spread, limit, cuts=(), kind=jnp.bfloat16):
    drawn = jax.random.normal(stream_key, dims, jnp.float32) * spread
    if len(cuts) > 0:
        drawn = level_of(stream_key, dims, cuts, -0.22, 0.18) * drawn
    return jnp.clip(drawn, min=-limit, max=limit).astype(kind)


def setup_inputs(seed: int = 0) -> dict:
    streams_of = jax.random.split(jax.random.key(seed), 8)
    qkv = draw_qkv(jax.random.fold_in(streams_of[7], 71), 0)
    gate = jnp.clip(0.5 + 2.0 * jax.random.uniform(streams_of[1], (CLIPS, D), jnp.float32) ** level_of(streams_of[1], (CLIPS, D), ((0, 8),), -0.2, 0.2), 0.5, 2.5)
    cotangent = bell_draw(streams_of[2], (CLIPS, SEQ, D), 1.0, 6.0, ((0, 8), (1, 4)))
    out_weight = bell_draw(streams_of[3], (HEADS * HD, D), (HEADS * HD) ** -0.5, 0.15625)
    clip_lengths = draw_clip_lengths(jax.random.fold_in(streams_of[7], 71), 0)
    text_lengths = draw_text_lengths(jax.random.fold_in(streams_of[7], 71), 0)
    plan = draw_plan(jax.random.fold_in(streams_of[7], 71), 0)
    return {"qkv": qkv, "gate": gate, "cotangent": cotangent, "out_weight": out_weight, "clip_lengths": clip_lengths, "text_lengths": text_lengths, "plan": plan}


NEGATIVE = -1e30


def allowed_rows(text_len, video_len):
    places = jnp.arange(SEQ, dtype=jnp.int32)
    return (places < text_len) | ((places >= TXT) & (places < TXT + video_len))


def reference(qkv, gate, cotangent, out_weight, clip_lengths, text_lengths, plan):
    head_width = HEADS * HD
    ordinal = jnp.arange(GROUPS, dtype=jnp.int32)
    inverse = jnp.zeros((GROUPS,), jnp.int32).at[plan].set(ordinal)
    source_of = jnp.stack([2 * ordinal, 2 * inverse + 1], axis=1).reshape(CLIPS).astype(jnp.int32)
    score_scale = HD ** -0.5

    def clip_step(weight_sum, inputs):
        tokens, gate_row, grad_row, text_len, video_len = inputs
        allowed = allowed_rows(text_len, video_len)
        live_pairs = (allowed[:, None] & allowed[None, :])[None]
        queries = tokens[:, :head_width].reshape(SEQ, HEADS, HD).astype(jnp.float32)
        keys_all = tokens[:, head_width:2 * head_width].reshape(SEQ, HEADS, HD).astype(jnp.float32)
        values_all = tokens[:, 2 * head_width:].reshape(SEQ, HEADS, HD).astype(jnp.float32)
        scores = jnp.einsum('qhd,khd->hqk', queries, keys_all) * score_scale
        masked = jnp.where(live_pairs, scores, NEGATIVE)
        row_peak = jnp.max(masked, axis=-1, keepdims=True)
        row_total = jnp.sum(jnp.exp(masked - row_peak), axis=-1, keepdims=True)
        log_total = row_peak + jnp.log(row_total)
        probabilities = jnp.exp(jnp.where(live_pairs, scores - log_total, NEGATIVE))
        probs_low = lax.optimization_barrier(probabilities.astype(jnp.bfloat16))
        attended = jnp.einsum('hqk,khd->qhd', probs_low.astype(jnp.float32), values_all).astype(jnp.bfloat16)
        attended = lax.optimization_barrier(attended)
        attended_flat = attended.reshape(SEQ, head_width)
        outputs = jnp.dot(attended_flat, out_weight, preferred_element_type=jnp.float32)
        mixed = (gate_row[None, :] * outputs).astype(jnp.bfloat16)
        gate_grad = jnp.sum(grad_row.astype(jnp.float32) * outputs, axis=0)
        scaled = (grad_row.astype(jnp.float32) * gate_row[None, :]).astype(jnp.bfloat16)
        weight_sum = weight_sum + jnp.dot(attended_flat.T, scaled, preferred_element_type=jnp.float32)
        d_attn = jnp.dot(scaled, out_weight.T, preferred_element_type=jnp.float32).astype(jnp.bfloat16)
        d_attn = lax.optimization_barrier(d_attn)
        d_heads = d_attn.reshape(SEQ, HEADS, HD).astype(jnp.float32)
        row_dots = jnp.einsum('qhd,qhd->hq', d_heads, attended.astype(jnp.float32))
        d_probs = jnp.einsum('qhd,khd->hqk', d_heads, values_all)
        d_scores = lax.optimization_barrier((probabilities * (d_probs - row_dots[..., None])).astype(jnp.bfloat16))
        d_scores = d_scores.astype(jnp.float32)
        grad_q = jnp.einsum('hqk,khd->qhd', d_scores, keys_all) * score_scale
        grad_k = jnp.einsum('hqk,qhd->khd', d_scores, queries) * score_scale
        grad_v = jnp.einsum('hqk,qhd->khd', probs_low.astype(jnp.float32), d_heads)
        gradients = jnp.concatenate([grad_q.reshape(SEQ, head_width), grad_k.reshape(SEQ, head_width), grad_v.reshape(SEQ, head_width)], axis=1).astype(jnp.bfloat16)
        return weight_sum, (mixed, gate_grad, gradients)

    scan_inputs = (qkv[source_of], gate, cotangent, text_lengths[source_of], clip_lengths[source_of])
    weight_grad, (mixed, gate_grad, balanced_grads) = lax.scan(clip_step, jnp.zeros((head_width, D), jnp.float32), scan_inputs)
    qkv_grad = jnp.zeros_like(qkv).at[source_of].set(balanced_grads)
    return mixed, gate_grad, weight_grad, qkv_grad
```

```python
import math

import jax
import jax.numpy as jnp
from jax import lax
from jax.experimental import pallas as pl
from jax.experimental.pallas import tpu as pltpu
from jax.sharding import PartitionSpec as P

HD = 128
TXT = 256
BLOCK = 256
NEGATIVE = -1e30
LOG2E = math.log2(math.e)


def dot(left, right, left_dim, right_dim):
    return lax.dot_general(
        left, right, (((left_dim,), (right_dim,)), ((), ())), preferred_element_type=jnp.float32
    )


def live_places(places, text_len, video_len):
    return (places < text_len) | ((places >= TXT) & (places < TXT + video_len))


def fill_bias(bias_ref, text_len, video_len):
    places = lax.broadcasted_iota(jnp.int32, bias_ref.shape, 0)
    bias_ref[...] = jnp.where(live_places(places, text_len, video_len), 0.0, NEGATIVE)


def forward_kernel(lens_ref, q_ref, k_ref, v_ref, out_ref, lse_ref, bias_ref):
    text_len, video_len = lens_ref[0], lens_ref[1]
    seq_len = q_ref.shape[0]
    score_scale = HD ** (-0.5) * LOG2E

    @pl.when(pl.program_id(0) == 0)
    def _():
        fill_bias(bias_ref, text_len, video_len)

    for block in range(seq_len // BLOCK):
        rows = pl.ds(block * BLOCK, BLOCK)
        scores = dot(k_ref[...], q_ref[rows, :], 1, 1) * score_scale + bias_ref[...]
        peak = jnp.max(scores, axis=0, keepdims=True)
        total = jnp.sum(jnp.exp2(scores - peak), axis=0, keepdims=True)
        places = block * BLOCK + lax.broadcasted_iota(jnp.int32, (1, BLOCK), 1)
        log_total = jnp.where(
            live_places(places, text_len, video_len), peak + jnp.log2(total), -NEGATIVE
        )
        lse_ref[0, :, rows] = log_total
        probs_low = jnp.exp2(scores - log_total).astype(jnp.bfloat16)
        out_ref[rows, :] = dot(v_ref[...], probs_low, 0, 0).T.astype(jnp.bfloat16)


def backward_kernel(
    lens_ref, q_ref, k_ref, v_ref, out_ref, d_ref, lse_ref,
    dq_ref, dk_ref, dv_ref, bias_ref, dk_sum, dv_sum,
):
    text_len, video_len = lens_ref[0], lens_ref[1]
    seq_len = q_ref.shape[0]
    score_scale = HD ** (-0.5)

    @pl.when(pl.program_id(0) == 0)
    def _():
        fill_bias(bias_ref, text_len, video_len)

    for block in range(seq_len // BLOCK):
        rows = pl.ds(block * BLOCK, BLOCK)
        q_rows = q_ref[rows, :]
        d_rows = d_ref[rows, :]
        products = d_rows.astype(jnp.float32) * out_ref[rows, :].astype(jnp.float32)
        row_dots = jnp.sum(products.T, axis=0, keepdims=True)
        scores = dot(k_ref[...], q_rows, 1, 1) * (score_scale * LOG2E) + bias_ref[...]
        probs = jnp.exp2(scores - lse_ref[0, :, rows])
        d_probs = dot(v_ref[...], d_rows, 1, 1)
        d_scores = (probs * (d_probs - row_dots)).astype(jnp.bfloat16)
        v_part = dot(probs.astype(jnp.bfloat16), d_rows, 1, 0)
        k_part = dot(d_scores, q_rows, 1, 0)
        q_part = dot(k_ref[...], d_scores, 0, 0).T
        dq_ref[rows, :] = (q_part * score_scale).astype(jnp.bfloat16)
        if block == 0:
            dk_sum[...] = k_part
            dv_sum[...] = v_part
        else:
            dk_sum[...] += k_part
            dv_sum[...] += v_part
    dk_ref[...] = (dk_sum[...] * score_scale).astype(jnp.bfloat16)
    dv_ref[...] = dv_sum[...].astype(jnp.bfloat16)


def head_spec(seq_len, first):
    return pl.BlockSpec((seq_len, HD), lambda head: (0, first + head))


def attend(lens, tokens):
    seq_len, width = tokens.shape
    heads = width // (3 * HD)
    work = heads * seq_len * seq_len
    return pl.pallas_call(
        forward_kernel,
        grid=(heads,),
        in_specs=[pl.BlockSpec(memory_space=pltpu.SMEM)]
        + [head_spec(seq_len, member * heads) for member in range(3)],
        out_specs=[
            head_spec(seq_len, 0),
            pl.BlockSpec((1, 1, seq_len), lambda head: (head, 0, 0)),
        ],
        out_shape=[
            jax.ShapeDtypeStruct((seq_len, heads * HD), jnp.bfloat16),
            jax.ShapeDtypeStruct((heads, 1, seq_len), jnp.float32),
        ],
        scratch_shapes=[pltpu.VMEM((seq_len, BLOCK), jnp.float32)],
        compiler_params=pltpu.CompilerParams(dimension_semantics=("arbitrary",)),
        cost_estimate=pl.CostEstimate(
            flops=8 * HD * work, bytes_accessed=8 * seq_len * width // 3, transcendentals=2 * work
        ),
        name="attend",
    )(lens, tokens, tokens, tokens)


def attend_back(lens, tokens, results, d_results, log_totals):
    seq_len, width = tokens.shape
    heads = width // (3 * HD)
    work = heads * seq_len * seq_len
    gradient = jax.ShapeDtypeStruct((seq_len, heads * HD), jnp.bfloat16)
    return pl.pallas_call(
        backward_kernel,
        grid=(heads,),
        in_specs=[pl.BlockSpec(memory_space=pltpu.SMEM)]
        + [head_spec(seq_len, member * heads) for member in range(3)]
        + [
            head_spec(seq_len, 0),
            head_spec(seq_len, 0),
            pl.BlockSpec((1, 1, seq_len), lambda head: (head, 0, 0)),
        ],
        out_specs=[head_spec(seq_len, 0)] * 3,
        out_shape=[gradient] * 3,
        scratch_shapes=[
            pltpu.VMEM((seq_len, BLOCK), jnp.float32),
            pltpu.VMEM((seq_len, HD), jnp.float32),
            pltpu.VMEM((seq_len, HD), jnp.float32),
        ],
        compiler_params=pltpu.CompilerParams(dimension_semantics=("arbitrary",)),
        cost_estimate=pl.CostEstimate(
            flops=20 * HD * work, bytes_accessed=16 * seq_len * width // 3, transcendentals=work
        ),
        name="attend_back",
    )(lens, tokens, tokens, tokens, results, d_results, log_totals)


def swap(blocks, axis):
    return lax.all_to_all(blocks, axis, split_axis=0, concat_axis=0, tiled=True)


def regroup(rows, order):
    groups = lax.axis_size("dp")
    spread = swap(rows.reshape(groups, rows.shape[0] // groups, rows.shape[1]), "dp")
    return swap(jnp.take(spread, order, axis=0), "dp").reshape(rows.shape)


def body(qkv, gate, cotangent, out_weight, clip_lengths, text_lengths, plan):
    groups = lax.axis_size("dp")
    ways = lax.axis_size("seq")
    ordinal = jnp.arange(groups, dtype=jnp.int32)
    inverse = jnp.sum(jnp.where(plan[None, :] == ordinal[:, None], ordinal[None, :], 0), axis=1)
    home_clip = 2 * lax.axis_index("dp")
    head_width, model_width = out_weight.shape
    local_width = head_width // ways
    rows = cotangent.shape[1]
    seq_len = rows * ways
    slots = (1, 0)

    lens, tokens = {}, {}
    for slot in slots:
        lens[slot] = jnp.stack([text_lengths[home_clip + slot], clip_lengths[home_clip + slot]])
        parted = qkv[slot].reshape(rows, 3, ways, local_width).transpose(2, 0, 1, 3)
        parted = parted.reshape(ways, rows, 3 * local_width)
        tokens[slot] = swap(parted, "seq").reshape(seq_len, 3 * local_width)

    results, log_totals, attn = {}, {}, {}
    for slot in slots:
        results[slot], log_totals[slot] = attend(lens[slot], tokens[slot])
        back = swap(results[slot].reshape(ways, rows, local_width), "seq")
        attn[slot] = back.transpose(1, 0, 2).reshape(rows, head_width)
    attn[1] = regroup(attn[1], inverse)

    mixed, gate_parts, scaled, grads = {}, {}, {}, {}
    for slot in (0, 1):
        outputs = jnp.dot(attn[slot], out_weight, preferred_element_type=jnp.float32)
        arriving = cotangent[slot].astype(jnp.float32)
        mixed[slot] = (gate[slot][None, :] * outputs).astype(jnp.bfloat16)
        gate_parts[slot] = jnp.sum(arriving * outputs, axis=0)
        scaled[slot] = (arriving * gate[slot][None, :]).astype(jnp.bfloat16)
        d_attn = dot(scaled[slot], out_weight, 1, 1).astype(jnp.bfloat16)
        if slot == 1:
            d_attn = regroup(d_attn, plan)
        d_parted = d_attn.reshape(rows, ways, local_width).transpose(1, 0, 2)
        d_heads = swap(d_parted, "seq").reshape(seq_len, local_width)
        parts = attend_back(lens[slot], tokens[slot], results[slot], d_heads, log_totals[slot])
        leaving = jnp.concatenate(parts, axis=1).reshape(ways, rows, 3 * local_width)
        landed = swap(leaving, "seq").reshape(ways, rows, 3, local_width)
        grads[slot] = landed.transpose(1, 2, 0, 3).reshape(rows, 3 * head_width)

    partial_weight = dot(
        jnp.concatenate([attn[0], attn[1]]), jnp.concatenate([scaled[0], scaled[1]]), 0, 0
    ).astype(jnp.bfloat16)
    group_weight = lax.psum_scatter(partial_weight, "dp", scatter_dimension=1, tiled=True)
    column_parts = group_weight.reshape(head_width, ways, -1).transpose(1, 0, 2)
    weight_grad = jnp.sum(swap(column_parts, "seq").astype(jnp.float32), axis=0)

    gate_part = jnp.stack([gate_parts[0], gate_parts[1]])
    gate_all = swap(jnp.broadcast_to(gate_part[None], (ways,) + gate_part.shape), "seq")
    gate_grad = jnp.sum(gate_all, axis=0)
    return (
        jnp.stack([mixed[0], mixed[1]]),
        gate_grad,
        weight_grad,
        jnp.stack([grads[0], grads[1]]),
    )


def solution(mesh):
    in_specs = (P("dp", "seq", None), P("dp", None), P("dp", "seq", None), P(), P(), P(), P())
    out_specs = (P("dp", "seq", None), P("dp", None), P(None, ("dp", "seq")), P("dp", "seq", None))
    return jax.shard_map(body, mesh=mesh, in_specs=in_specs, out_specs=out_specs, check_vma=False)
```
